512 devices in a mesh: dom: 8 (over y_hi, core), fsdp: 64 (over x, z, y_lo).
Axes of the slice: x: 4, y: 8 (y_hi: 4, y_lo: 2; y = y_hi * 2 + y_lo), z: 8, core: 2. Of those that a mesh axis runs over, the one named last changes fastest.
Arguments:
- weights: bfloat16 [8, 64, 640, 896], P('dom', 'fsdp'), may hold values from -6 to 6
- activations: bfloat16 [8, 2, 1280, 2560], P('dom', None, 'fsdp'), may hold values from -6 to 6
- cotangents: bfloat16 [8, 2, 1280, 14336], P('dom', None, 'fsdp'), may hold values from -0.15625 to 0.15625
- lengths: int32 [8, 2, 64], P('dom', None, 'fsdp'), may hold values from 1 to 20, 960 in all within a row
Outputs:
- merged: bfloat16 [64, 640, 896], P('fsdp')
The draws below stay inside these ranges and needn't reach their ends.
Inputs may be any that keep to these rules, and one draw needn't show every extreme that they name: In every domain and micro-batch the lengths sum to 960, and some block is full.
All inputs are finite; a program needn't handle non-finite values.
Results may differ from the reference program's by a relative error of at most 0.018.
Values may be sent and summed in bfloat16 or wider, within the bound.
No kernel may reach another device: no remote copies, remote signals or barrier semaphores. Data moves between devices by JAX's collectives and lax.ppermute only.
A program may use at most 64 MiB of HBM per device.

```python
import math
import jax
import jax.numpy as jnp
import numpy as np
from jax import lax

D = 2560
F = 14336
MB = 2
RB = 4
SLOTS = 20
CB = 16
TR = 640
TC = 896
TILES = 64
DOMAINS = 8
TOKENS = 1280
N_FSDP = 64


def steps_of(own_key, dims, cuts, smallest, largest):
    def one(axis_at, blocks):
        steps = jax.random.uniform(jax.random.fold_in(jax.random.fold_in(own_key, 6), axis_at), (blocks,), jnp.float32, smallest / len(cuts), largest / len(cuts))
        return jnp.repeat(jnp.exp(steps), dims[axis_at] // blocks).reshape((-1,) + (1,) * (len(dims) - axis_at - 1))

    level = one(*cuts[0])
    for cut in cuts[1:]:
        level = level * one(*cut)
    return level


def split_up(count, total, most, skew):
    weights = [(1 << 20) // math.isqrt(grade ** skew) + 1 for grade in range(2, count + 1)]
    surplus, holding = total - most - (count - 1), [1] * (count - 1)
    while surplus > 0:
        candidates = [i for i in range(count - 1) if holding[i] < most]
        whole, remaining = sum([weights[i] for i in candidates]), surplus
        for i in candidates:
            extra = min(most - holding[i], max(1, remaining * weights[i] // whole), surplus)
            holding[i] = holding[i] + extra
            surplus = surplus - extra
    return np.array([most] + holding)


def ragged(rng, count, total, reach, lean):
    if count == 2:
        one = jax.random.randint(rng, (), max(1, total - reach), min(reach, total - 1) + 1)
        return jnp.stack([one, total - one])
    tallies = jnp.asarray(split_up(count, total, reach, lean), jnp.int32)
    pairs = (count - 1) // 2
    giver, taker = tallies[1:1 + 2 * pairs:2], tallies[2:2 + 2 * pairs:2]
    slack = jnp.minimum(giver - 1, reach - taker)
    moved = jax.random.randint(jax.random.fold_in(rng, 1), (pairs,), 0, 1 << 20) % (slack + 1)
    tallies = tallies.at[1:1 + 2 * pairs:2].set(giver - moved).at[2:2 + 2 * pairs:2].set(taker + moved)
    return tallies[jax.random.permutation(jax.random.fold_in(rng, 2), count)]


def centred(own_key, extent, scale, limit, split=(), kind=jnp.bfloat16):
    drawn = jax.random.normal(own_key, extent, jnp.float32) * scale
    if len(split) > 0:
        drawn = steps_of(own_key, extent, split, -0.22, 0.18) * drawn
    return jnp.clip(drawn, min=-limit, max=limit).astype(kind)


def setup_inputs(seed: int = 0) -> dict:
    splits = jax.random.split(jax.random.key(seed), 5)
    weights = centred(splits[0], (DOMAINS, TILES, TR, TC), 1.0, 6.0, ((0, 8), (1, 64)))
    activations = centred(splits[1], (DOMAINS, MB, TOKENS, D), 1.0, 6.0, ((0, 8), (2, 64)))
    cotangents = centred(splits[2], (DOMAINS, MB, TOKENS, F), TOKENS ** -0.5, 0.15625, ((0, 8), (2, 64)))
    lengths = jax.vmap(lambda own: ragged(own, N_FSDP, 3 * SLOTS * N_FSDP // 4, SLOTS, 2))(jax.random.split(splits[3], DOMAINS * MB)).reshape((DOMAINS, MB, N_FSDP)).astype(jnp.int32)
    return dict(weights=weights, activations=activations, cotangents=cotangents, lengths=lengths)


damping = 0.001


def domain_terms(weight, feats, cots, lens):
    pos = jnp.arange(TOKENS) % SLOTS
    owner = jnp.arange(TOKENS) // SLOTS
    fisher = jnp.zeros((D, F), jnp.float32)
    for step in range(MB):
        mask = (pos < lens[step][owner]).astype(jnp.bfloat16)
        masked = feats[step] * mask[:, None]
        grad = jnp.dot(masked.T, cots[step], preferred_element_type=jnp.float32)
        fisher = fisher + grad * grad
    fisher = fisher / MB
    tiled = fisher.reshape(RB, TR, CB, TC).transpose(0, 2, 1, 3).reshape(TILES, TR, TC)
    term = tiled + damping
    numer_term = (term * weight.astype(jnp.float32)).astype(jnp.bfloat16)
    denom_term = term.astype(jnp.bfloat16)
    return numer_term, denom_term


def reference(weights, activations, cotangents, lengths):
    def accumulate(carry, idx):
        numer_term, denom_term = domain_terms(weights[idx], activations[idx], cotangents[idx], lengths[idx])
        return (carry[0] + numer_term.astype(jnp.float32), carry[1] + denom_term.astype(jnp.float32)), None

    start = (jnp.zeros((TILES, TR, TC), jnp.float32), jnp.zeros((TILES, TR, TC), jnp.float32))
    (numer, denom), unused = lax.scan(accumulate, start, jnp.arange(DOMAINS))
    return (numer / denom).astype(jnp.bfloat16)
```

```python
import jax
import jax.numpy as jnp
from jax import lax
from jax.sharding import Mesh, PartitionSpec as P

damping = 0.001
axes = ("yhi", "core", "x", "z", "ylo")


def shift(value, axis, by):
    count = lax.axis_size(axis)
    return lax.ppermute(value, axis, [(i, (i + by) % count) for i in range(count)])


def exchange(value, axis):
    return lax.all_to_all(value, axis, split_axis=0, concat_axis=0, tiled=True)


def put(whole, piece, dim, index, split=None, start=0):
    at = [0] * whole.ndim
    at[dim] = index % whole.shape[dim]
    if split is not None:
        at[split] = start
    return lax.dynamic_update_slice(whole, jnp.expand_dims(piece, dim), at)


def room(own, axis, dim):
    shape = list(own.shape)
    shape.insert(dim, lax.axis_size(axis))
    return jnp.zeros(shape, own.dtype)


def body(weights, activations, cotangents, lengths):
    xs, zs, ys = (lax.axis_size(a) for a in ("x", "z", "ylo"))
    cores, his = lax.axis_size("core"), lax.axis_size("yhi")
    x, z, y, core = (lax.axis_index(a) for a in ("x", "z", "ylo", "core"))
    rows, cols = weights.shape[2:]
    batches, slots = activations.shape[1:3]

    cots = cotangents[0].reshape(batches, slots, zs * ys, cols).transpose(2, 0, 1, 3)
    cots = exchange(cots, ("z", "ylo"))
    cots = cots.reshape(zs, ys, batches, slots, cols).transpose(2, 0, 1, 3, 4).reshape(batches, zs, ys * slots, cols)

    mask = (jnp.arange(slots)[None, :] < lengths[0, :, 0:1]).astype(jnp.bfloat16)
    feats = (activations[0] * mask[:, :, None]).reshape(batches, slots, xs, rows).transpose(2, 0, 1, 3)
    own = lax.dynamic_index_in_dim(feats, x, 0, keepdims=False)
    plane = put(room(own, "x", 1), own, 1, x)
    for k in range(1, xs):
        block = lax.dynamic_index_in_dim(feats, (x + k) % xs, 0, keepdims=False)
        plane = put(plane, shift(block, "x", k), 1, x - k)
    pair = put(room(plane, "ylo", 2), plane, 2, y)
    pair = put(pair, shift(plane, "ylo", 1), 2, 1 - y)
    own = pair.reshape(batches, xs * ys * slots, rows)

    whole = put(room(own, "z", 1), own, 1, z)
    up = down = own
    for k in range(1, zs // 2):
        up, down = shift(up, "z", 1), shift(down, "z", -1)
        whole = put(put(whole, up, 1, z - k), down, 1, z + k)
    down = shift(down, "z", -1)
    feats = put(whole, down, 1, z + zs // 2).reshape(batches, -1, rows)

    whole = put(room(cots, "x", 2), cots, 2, x)
    up, down = shift(cots, "x", 1), shift(cots, "x", -1)
    whole = put(put(whole, up, 2, x - 1), down, 2, x + 1)
    half = zs // 2
    up, down = shift(up[:, :half], "x", 1), shift(down[:, half:], "x", -1)
    whole = put(put(whole, up, 2, x + 2), down, 2, x + 2, 1, half)
    cots = whole.reshape(batches, -1, cols)

    grad = jnp.einsum("mkr,mkc->mrc", feats, cots, preferred_element_type=jnp.float32)
    term = jnp.sum(grad * grad, axis=0) / batches + damping
    numer = (term * weights[0, 0].astype(jnp.float32)).astype(jnp.bfloat16)
    terms = jnp.stack([numer, term.astype(jnp.bfloat16)])
    terms = terms.reshape(2, cores, his, rows // cores // his, cols)
    other = shift(lax.dynamic_index_in_dim(terms, 1 - core, 1, keepdims=False), "core", 1)
    mine = lax.dynamic_index_in_dim(terms, core, 1, keepdims=False)
    both = (mine.astype(jnp.float32) + other.astype(jnp.float32)).astype(jnp.bfloat16)
    both = exchange(both.transpose(1, 0, 2, 3), "yhi")
    sums = jnp.sum(both.astype(jnp.float32), axis=0)
    merged = (sums[0] / sums[1]).astype(jnp.bfloat16)
    merged = exchange(jnp.broadcast_to(merged[None], (his,) + merged.shape), "yhi")
    merged = merged.reshape(rows // cores, cols)
    other = shift(merged, "core", 1)
    out = jnp.where(core == 0, jnp.stack([merged, other]), jnp.stack([other, merged]))
    return out.reshape(1, rows, cols)


def solution(mesh):
    inner = Mesh(mesh.devices.reshape(4, 2, 4, 8, 2), axes)
    dom, fsdp = axes[:2], axes[2:]
    return jax.shard_map(
        body,
        mesh=inner,
        in_specs=(
            P(dom, fsdp, None, None),
            P(dom, None, fsdp, None),
            P(dom, None, fsdp, None),
            P(dom, None, fsdp),
        ),
        out_specs=P(fsdp, None, None),
        check_vma=False,
    )
```

```python
import functools

import jax
import jax.numpy as jnp
from jax import lax
from jax.experimental import pallas as pl
from jax.experimental.layout import Layout, with_layout_constraint
from jax.experimental.pallas import tpu as pltpu
from jax.sharding import Mesh, PartitionSpec as P

damping = 0.001
axes = ("yhi", "core", "x", "z", "ylo")
far = (2, 1, 3)
back = (1, 3, 2)


def shift(value, axis, by):
    count = lax.axis_size(axis)
    return lax.ppermute(value, axis, [(i, (i + by) % count) for i in range(count)])


def exchange(value, axis):
    return lax.all_to_all(value, axis, split_axis=0, concat_axis=0, tiled=True)


def put(whole, piece, dim, index, split=None, start=0):
    at = [0] * whole.ndim
    at[dim] = index % whole.shape[dim]
    if split is not None:
        at[split] = start
    return lax.dynamic_update_slice(whole, jnp.expand_dims(piece, dim), at)


def plain(value):
    return with_layout_constraint(value, Layout(major_to_minor=tuple(range(value.ndim))))


def room(own, axis, dim):
    shape = list(own.shape)
    shape.insert(dim, lax.axis_size(axis))
    return jnp.zeros(shape, own.dtype)


def product(feats, cots, m):
    lhs = feats[m].reshape(-1, feats.shape[-1])
    rhs = cots[m].reshape(-1, cots.shape[-1])
    return lax.dot_general(lhs, rhs, (((0,), (0,)), ((), ())), preferred_element_type=jnp.float32)


def run(copies, sems):
    made = [pltpu.make_async_copy(source, target, sems.at[i]) for i, (source, target) in enumerate(copies)]
    for copy in made:
        copy.start()
    return made


def early_kernel(count, where, *refs):
    feat_refs, cot_refs, (out, feats, cots, sems) = refs[:count], refs[count:-4], refs[-4:]
    near = len(cot_refs)
    copies = [(ref.at[:, :near], feats.at[:, :, where[i]]) for i, ref in enumerate(feat_refs)]
    copies += [(ref, cots.at[:, i]) for i, ref in enumerate(cot_refs)]
    made = run(copies, sems)
    missing = jnp.zeros(feats.shape[3:], feats.dtype)
    for m in range(out.shape[0]):
        for i in range(near):
            feats[m, i, where[count]] = missing
    for copy in made:
        copy.wait()
    for m in range(out.shape[0]):
        out[m] = product(feats, cots, m)


def late_kernel(count, where, *refs):
    feat_refs, (*near_refs, low, high, partial, weight) = refs[:count], refs[count:-8]
    mine, theirs, feats, cots, held, scale, sems, more = refs[-8:]
    batches, rows = held.shape[:2]
    half, near, zs = low.shape[1], len(near_refs), 2 * low.shape[1]
    copies = [(low, cots.at[:, :half]), (high, cots.at[:, half:zs])]
    copies += [(ref.at[:, near], feats.at[:, where[i]]) for i, ref in enumerate(feat_refs)]
    copies += [(feat_refs[-1].at[:, :near], feats.at[:, zs:])]
    copies += [(ref.at[:, where[count - 1]], cots.at[:, zs + i]) for i, ref in enumerate(near_refs)]
    first = run(copies, sems)
    second = run([(partial, held), (weight, scale)], more)
    for copy in first:
        copy.wait()
    grads = [product(feats, cots, m) for m in range(batches)]
    for copy in second:
        copy.wait()
    for side in range(2):
        part = slice(side * rows // 2, (side + 1) * rows // 2)
        total = 0.0
        for m in range(batches):
            grad = held[m, part, :] + grads[m][part]
            total = total + grad * grad
        term = total / batches + damping
        numer = (term * scale[part, :].astype(jnp.float32)).astype(jnp.bfloat16)
        denom = term.astype(jnp.bfloat16)

        @pl.when(where[count] == side)
        def _(numer=numer, denom=denom):
            mine[0], mine[1] = numer, denom

        @pl.when(where[count] != side)
        def _(numer=numer, denom=denom):
            theirs[0], theirs[1] = numer, denom


def call(kernel, where, feats, others, out, scratch, flops):
    hbm, vmem = pl.BlockSpec(memory_space=pl.ANY), pl.BlockSpec(memory_space=pltpu.VMEM)
    return pl.pallas_call(
        functools.partial(kernel, len(feats)),
        out_shape=out,
        in_specs=[pl.BlockSpec(memory_space=pltpu.SMEM)] + [hbm] * (len(feats) + len(others)),
        out_specs=jax.tree.map(lambda _: vmem, out),
        scratch_shapes=scratch,
        cost_estimate=pl.CostEstimate(flops=flops, bytes_accessed=12 << 20, transcendentals=0),
        compiler_params=pltpu.CompilerParams(vmem_limit_bytes=56 << 20),
    )(where, *feats, *others)


def early_call(where, feats, cots):
    batches, zs, used, cols = cots[0].shape
    rows, near = feats[0].shape[3], len(cots)
    out = jax.ShapeDtypeStruct((batches, rows, cols), jnp.float32)
    scratch = [
        pltpu.VMEM((batches, near, zs, used, rows), jnp.bfloat16),
        pltpu.VMEM((batches, near, zs, used, cols), jnp.bfloat16),
        pltpu.SemaphoreType.DMA((len(feats) + near,)),
    ]
    return call(early_kernel, where, feats, cots, out, scratch, 2 * batches * near * zs * used * rows * cols)


def late_call(where, feats, cots, low, high, partial, weight):
    batches, zs, used, cols = cots[0].shape
    rows, near = feats[0].shape[3], len(cots)
    out = jax.ShapeDtypeStruct((2, rows // 2, cols), jnp.bfloat16)
    scratch = [
        pltpu.VMEM((batches, zs + near, used, rows), jnp.bfloat16),
        pltpu.VMEM((batches, zs + near, used, cols), jnp.bfloat16),
        pltpu.VMEM((batches, rows, cols), jnp.float32),
        pltpu.VMEM((rows, cols), jnp.bfloat16),
        pltpu.SemaphoreType.DMA((len(feats) + near + 3,)),
        pltpu.SemaphoreType.DMA((2,)),
    ]
    others = [*cots, low, high, partial, weight]
    flops = 2 * batches * (zs + near) * used * rows * cols
    return call(late_kernel, where, feats, others, (out, out), scratch, flops)


def body(weights, activations, cotangents, lengths):
    xs, zs, ys = (lax.axis_size(a) for a in ("x", "z", "ylo"))
    cores, his = lax.axis_size("core"), lax.axis_size("yhi")
    x, z, y, core = (lax.axis_index(a) for a in ("x", "z", "ylo", "core"))
    rows, cols = weights.shape[2:]
    batches, slots = activations.shape[1:3]

    cots = cotangents[0].transpose(1, 0, 2).reshape(slots, batches, zs * ys, cols).transpose(2, 0, 1, 3)
    cots = exchange(cots, ("z", "ylo"))
    cots = cots.transpose(2, 0, 1, 3).reshape(batches, zs, ys * slots, cols)

    mask = (jnp.arange(slots)[None, :] < lengths[0, :, 0:1]).astype(jnp.bfloat16)
    feats = activations[0] * mask[:, :, None]
    feats = feats.transpose(1, 0, 2).reshape(slots, batches, xs, rows).transpose(2, 0, 1, 3)
    blocks = [lax.dynamic_index_in_dim(feats, (x + k) % xs, 0, keepdims=False) for k in range(xs)]
    plane = plain(jnp.stack([blocks[0]] + [shift(blocks[k], "x", k) for k in back]))
    pair = put(room(plane, "ylo", 1), plane, 1, y)
    pair = plain(put(pair, shift(plane, "ylo", 1), 1, 1 - y))
    own = pair.transpose(3, 0, 1, 2, 4).reshape(batches, xs, ys * slots, rows)

    up = down = own
    pieces, places = [own], [0]
    for k in range(1, zs // 2):
        up, down = shift(up, "z", 1), shift(down, "z", -1)
        pieces, places = pieces + [up, down], places + [-k, k]
    pieces, places = pieces + [shift(down, "z", -1)], places + [zs // 2]

    half = zs // 2
    left, right = shift(cots, "x", 1), shift(cots, "x", -1)
    first, second = shift(left[:, :half], "x", 1), shift(right[:, half:], "x", -1)

    zat = [(z + at) % zs for at in places]
    near = [cots, left, right]
    partial = early_call(jnp.stack(zat).astype(jnp.int32), pieces[:-1], near)
    where = jnp.stack(zat + [core]).astype(jnp.int32)
    mine, theirs = late_call(where, pieces, near, first, second, partial, weights[0, 0])
    other = shift(theirs, "core", 1)
    both = (mine.astype(jnp.float32) + other.astype(jnp.float32)).astype(jnp.bfloat16)
    both = both.reshape(2, his, rows // cores // his, cols).transpose(1, 0, 2, 3)
    high = lax.axis_index("yhi")
    sums = lax.dynamic_index_in_dim(both, high, 0, keepdims=False).astype(jnp.float32)
    parts = [lax.dynamic_index_in_dim(both, (high + k) % his, 0, keepdims=False) for k in far]
    for k, part in zip(far, parts):
        sums = sums + shift(part, "yhi", k).astype(jnp.float32)
    merged = (sums[0] / sums[1]).astype(jnp.bfloat16)
    merged = exchange(jnp.broadcast_to(merged[None], (his,) + merged.shape), "yhi")
    merged = merged.reshape(rows // cores, cols)
    other = shift(merged, "core", 1)
    out = jnp.where(core == 0, jnp.stack([merged, other]), jnp.stack([other, merged]))
    return out.reshape(1, rows, cols)


def solution(mesh):
    inner = Mesh(mesh.devices.reshape(4, 2, 4, 8, 2), axes)
    dom, fsdp = axes[:2], axes[2:]
    return jax.shard_map(
        body,
        mesh=inner,
        in_specs=(
            P(dom, fsdp, None, None),
            P(dom, None, fsdp, None),
            P(dom, None, fsdp, None),
            P(dom, None, fsdp),
        ),
        out_specs=P(fsdp, None, None),
        check_vma=False,
    )
```

```python
import functools

import jax
import jax.numpy as jnp
from jax import lax
from jax.experimental import pallas as pl
from jax.experimental.layout import Layout, with_layout_constraint
from jax.experimental.pallas import tpu as pltpu
from jax.sharding import Mesh, PartitionSpec as P

damping = 0.001
axes = ("yhi", "core", "x", "z", "ylo")
back = (1, 3, 2)


def shift(value, axis, by):
    count = lax.axis_size(axis)
    return lax.ppermute(value, axis, [(i, (i + by) % count) for i in range(count)])


def exchange(value, axis):
    return lax.all_to_all(value, axis, split_axis=0, concat_axis=0, tiled=True)


def put(whole, piece, dim, index, split=None, start=0):
    at = [0] * whole.ndim
    at[dim] = index % whole.shape[dim]
    if split is not None:
        at[split] = start
    return lax.dynamic_update_slice(whole, jnp.expand_dims(piece, dim), at)


def plain(value):
    return with_layout_constraint(value, Layout(major_to_minor=tuple(range(value.ndim))))


def room(own, axis, dim):
    shape = list(own.shape)
    shape.insert(dim, lax.axis_size(axis))
    return jnp.zeros(shape, own.dtype)


def product(feats, cots, m):
    lhs = feats[m].reshape(-1, feats.shape[-1])
    rhs = cots[m].reshape(-1, cots.shape[-1])
    return lax.dot_general(lhs, rhs, (((0,), (0,)), ((), ())), preferred_element_type=jnp.float32)


def run(copies, sems):
    made = [pltpu.make_async_copy(source, target, sems.at[i]) for i, (source, target) in enumerate(copies)]
    for copy in made:
        copy.start()
    return made


def early_kernel(count, where, *refs):
    feat_refs, cot_refs, (out, feats, cots, sems) = refs[:count], refs[count:-4], refs[-4:]
    near = len(cot_refs)
    copies = [(ref.at[:, :near], feats.at[:, :, where[i]]) for i, ref in enumerate(feat_refs)]
    copies += [(ref, cots.at[:, i]) for i, ref in enumerate(cot_refs)]
    made = run(copies, sems)
    missing = jnp.zeros(feats.shape[3:], feats.dtype)
    for m in range(out.shape[0]):
        for i in range(near):
            feats[m, i, where[count]] = missing
    for copy in made:
        copy.wait()
    for m in range(out.shape[0]):
        out[m] = product(feats, cots, m)


def late_kernel(count, where, *refs):
    feat_refs, (*near_refs, low, high, held) = refs[:count], refs[count:-4]
    out, feats, cots, sems = refs[-4:]
    batches, _ = held.shape[:2]
    half, near, zs = low.shape[1], len(near_refs), 2 * low.shape[1]
    copies = [(low, cots.at[:, :half]), (high, cots.at[:, half:zs])]
    copies += [(ref.at[:, near], feats.at[:, where[i]]) for i, ref in enumerate(feat_refs)]
    copies += [(feat_refs[-1].at[:, :near], feats.at[:, zs:])]
    copies += [(ref.at[:, where[count - 1]], cots.at[:, zs + i]) for i, ref in enumerate(near_refs)]
    for copy in run(copies, sems):
        copy.wait()
    grads = [product(feats, cots, m) for m in range(batches)]
    total = 0.0
    for m in range(batches):
        grad = held[m] + grads[m]
        total = total + grad * grad
    out[...] = (total / batches + damping).astype(out.dtype)


def call(kernel, where, feats, others, inside, out, scratch, flops):
    hbm, vmem = pl.BlockSpec(memory_space=pl.ANY), pl.BlockSpec(memory_space=pltpu.VMEM)
    return pl.pallas_call(
        functools.partial(kernel, len(feats)),
        out_shape=out,
        in_specs=[pl.BlockSpec(memory_space=pltpu.SMEM)] + [hbm] * (len(feats) + len(others)) + [vmem] * len(inside),
        out_specs=jax.tree.map(lambda _: vmem, out),
        scratch_shapes=scratch,
        cost_estimate=pl.CostEstimate(flops=flops, bytes_accessed=12 << 20, transcendentals=0),
        compiler_params=pltpu.CompilerParams(vmem_limit_bytes=28 << 20),
    )(where, *feats, *others, *inside)


def early_call(where, feats, cots):
    batches, zs, used, cols = cots[0].shape
    rows, near = feats[0].shape[3], len(cots)
    out = jax.ShapeDtypeStruct((batches, rows, cols), jnp.float32)
    scratch = [
        pltpu.VMEM((batches, near, zs, used, rows), jnp.bfloat16),
        pltpu.VMEM((batches, near, zs, used, cols), jnp.bfloat16),
        pltpu.SemaphoreType.DMA((len(feats) + near,)),
    ]
    return call(early_kernel, where, feats, cots, [], out, scratch, 2 * batches * near * zs * used * rows * cols)


def late_call(where, feats, cots, low, high, partial):
    batches, zs, used, cols = cots[0].shape
    rows, near = feats[0].shape[3], len(cots)
    out = jax.ShapeDtypeStruct((rows, cols), jnp.bfloat16)
    scratch = [
        pltpu.VMEM((batches, zs + near, used, rows), jnp.bfloat16),
        pltpu.VMEM((batches, zs + near, used, cols), jnp.bfloat16),
        pltpu.SemaphoreType.DMA((len(feats) + near + 3,)),
    ]
    others, inside = [*cots, low, high], [partial]
    flops = 2 * batches * (zs + near) * used * rows * cols
    return call(late_kernel, where, feats, others, inside, out, scratch, flops)


def body(weights, activations, cotangents, lengths):
    xs, zs, ys = (lax.axis_size(a) for a in ("x", "z", "ylo"))
    cores, his = lax.axis_size("core"), lax.axis_size("yhi")
    x, z, y, core = (lax.axis_index(a) for a in ("x", "z", "ylo", "core"))
    rows, cols = weights.shape[2:]
    batches, slots = activations.shape[1:3]

    cots = cotangents[0].transpose(1, 0, 2).reshape(slots, batches, zs * ys, cols).transpose(2, 0, 1, 3)
    cots = exchange(cots, ("z", "ylo"))
    cots = cots.transpose(2, 0, 1, 3).reshape(batches, zs, ys * slots, cols)

    mask = (jnp.arange(slots)[None, :] < lengths[0, :, 0:1]).astype(jnp.bfloat16)
    feats = activations[0] * mask[:, :, None]
    feats = feats.transpose(1, 0, 2).reshape(slots, batches, xs, rows).transpose(2, 0, 1, 3)
    blocks = [lax.dynamic_index_in_dim(feats, (x + k) % xs, 0, keepdims=False) for k in range(xs)]
    plane = plain(jnp.stack([blocks[0]] + [shift(blocks[k], "x", k) for k in back]))
    pair = put(room(plane, "ylo", 1), plane, 1, y)
    pair = plain(put(pair, shift(plane, "ylo", 1), 1, 1 - y))
    own = pair.transpose(3, 0, 1, 2, 4).reshape(batches, xs, ys * slots, rows)

    up = down = own
    pieces, places = [own], [0]
    for k in range(1, zs // 2):
        up, down = shift(up, "z", 1), shift(down, "z", -1)
        pieces, places = pieces + [up, down], places + [-k, k]
    pieces, places = pieces + [shift(down, "z", -1)], places + [zs // 2]

    half = zs // 2
    left, right = shift(cots, "x", 1), shift(cots, "x", -1)
    first, second = shift(left[:, :half], "x", 1), shift(right[:, half:], "x", -1)

    where = jnp.append((z + jnp.asarray(places)) % zs, core).astype(jnp.int32)
    near = [cots, left, right]
    partial = early_call(where, pieces[:-1], near)
    term = late_call(where, pieces, near, first, second, partial)
    part = rows // (cores * his)
    others = exchange(weights.reshape(his * cores, part, cols), ("yhi", "core")).astype(jnp.float32)
    terms = exchange(term.reshape(his * cores, part, cols), ("yhi", "core")).astype(jnp.float32)
    merged = (jnp.sum(terms * others, axis=0) / jnp.sum(terms, axis=0)).astype(jnp.bfloat16)
    merged = exchange(jnp.broadcast_to(merged[None], (his,) + merged.shape), "yhi")
    other = shift(merged, "core", 1)
    out = jnp.where(core == 0, jnp.stack([merged, other], 1), jnp.stack([other, merged], 1))
    return out.reshape(1, rows, cols)


def solution(mesh):
    inner = Mesh(mesh.devices.reshape(4, 2, 4, 8, 2), axes)
    dom, fsdp = axes[:2], axes[2:]
    return jax.shard_map(
        body,
        mesh=inner,
        in_specs=(
            P(dom, fsdp, None, None),
            P(dom, None, fsdp, None),
            P(dom, None, fsdp, None),
            P(dom, None, fsdp),
        ),
        out_specs=P(fsdp, None, None),
        check_vma=False,
    )
```
